32 devices in a mesh: dp: 2 (over y), expert: 4 (over x, core), tensor: 4 (over z).
Axes of the slice: x: 2, y: 2, z: 4, core: 2. Of those that a mesh axis runs over, the one named last changes fastest.
Arguments:
- hidden_states: bfloat16 [256, 4096], P(('dp', 'expert'), 'tensor'), may hold values from -6 to 6
- chosen_experts: int32 [256, 2], P(('dp', 'expert')), may hold values from 0 to 3, all different within a row; in each aligned block of 32 rows (0 to 31, 32 to 63, ...) at most 16 rows name the same one
- choice_weights: float32 [256, 2], P(('dp', 'expert')), may hold values from 0.2 to 1
- gate_proj: bfloat16 [4, 4096, 8192], P('expert', None, ('dp', 'tensor')), may hold values from -0.09375 to 0.09375
- up_proj: bfloat16 [4, 4096, 8192], P('expert', None, ('dp', 'tensor')), may hold values from -0.09375 to 0.09375
- down_proj: bfloat16 [4, 8192, 4096], P('expert', 'dp', 'tensor'), may hold values from -0.0625 to 0.0625
Outputs:
- moe_output: bfloat16 [256, 4096], P(('dp', 'expert'), 'tensor')
The draws below stay inside these ranges and needn't reach their ends.
Inputs may be any that keep to these rules, and one draw needn't show every extreme that they name: `chosen_experts`: each row names 2 different experts; among the 32 rows of one device no expert is named more than 16 times, a bound that some block reaches.
All inputs are finite; a program needn't handle non-finite values.
Results may differ from the reference program's by a relative error of at most 0.0058.
Values may be sent and summed in bfloat16 or wider, within the bound.
A program may use at most 64 MiB of HBM per device.

```python
import math
import jax
import jax.numpy as jnp
import numpy as np
from jax import lax

D = 4096
FF = 8192
TOP = 2
CAP = 16
TOK_DEV = 32
EXPERTS = 4
TOKENS = 256
N_DP = 2


def steps_of(stream_key, extent, pieces, least, largest):
    factor_of = 1.0
    for dim, parts in pieces:
        heights = jax.random.uniform(jax.random.fold_in(jax.random.fold_in(stream_key, 6), dim), (parts,), jnp.float32, least / len(pieces), largest / len(pieces))
        factor_of = factor_of * jnp.repeat(jnp.exp(heights), extent[dim] // parts).reshape((-1,) + (1,) * (len(extent) - 1 - dim))
    return factor_of


def assign_block(key, own, number, rows, number_of, top, bound, slope):
    order = jax.random.permutation(key, number_of)
    packed, common = shares(number_of, rows * top, bound, slope, True), shares(number_of, rows * top, bound, slope, False)
    places = jnp.arange(number_of)

    def named(sizes, offset_by):
        used = int((sizes > 0).sum())
        fixed = max(1, used // 4)
        passed = fixed + (places - fixed + offset_by * (used - fixed)) % max(1, number_of - fixed)
        return jnp.zeros((number_of,), jnp.int32).at[order[jnp.where(places < fixed, places, passed)]].set(jnp.asarray(sizes, jnp.int32))

    sizes = jnp.where(number % 4 == 0, named(packed, number // 4), named(common, number - number // 4 - 1))
    mixed = jax.random.permutation(jax.random.fold_in(own, 3), number_of)
    source_of, taker = mixed[0:number_of // 2 * 2:2], mixed[1:number_of // 2 * 2:2]
    room = jnp.minimum(sizes[source_of] - 1, bound - sizes[taker]) // 2
    room = jnp.where((source_of == order[0]) | (taker == order[0]) | (sizes[taker] == 0), 0, jnp.maximum(room, 0))
    passed = jax.random.randint(jax.random.fold_in(own, 4), (number_of // 2,), 0, 1 << 20) % (room + 1)
    sizes = sizes.at[source_of].add(-passed).at[taker].add(passed)
    items = jnp.searchsorted(jnp.cumsum(sizes), jnp.arange(rows * top), side="right").astype(jnp.int32)
    table = items.reshape(top, rows).T
    table = table[jax.random.permutation(jax.random.fold_in(own, 1), rows)]
    offset_by = jax.random.randint(jax.random.fold_in(own, 2), (rows, 1), 0, top)
    return jnp.take_along_axis(table, (jnp.arange(top)[None, :] + offset_by) % top, axis=1)


def shares(number_of, total, most, skew, full):
    weights = [(1 << 20) // math.isqrt(standing ** skew) + 1 for standing in range(1, number_of + 1)]
    largest = most if full else min(most, max(-(-total // number_of), total * weights[0] // sum(weights)))
    least = 1 if total - largest >= number_of - 1 else 0
    given, spare = [largest] + [least] * (number_of - 1), total - largest - least * (number_of - 1)
    while spare > 0:
        candidates = [i for i in range(1, number_of) if given[i] < largest] or [i for i in range(1, number_of) if given[i] < most]
        pool, remaining = sum([weights[i] for i in candidates]), spare
        for i in candidates:
            more = min(most - given[i], max(1, remaining * weights[i] // pool), spare)
            given[i] = given[i] + more
            spare = spare - more
    return np.array(given)


def centred(key, extent, deviation, limit, cuts=(), kind=jnp.bfloat16):
    array = jax.random.normal(key, extent, jnp.float32) * deviation
    if len(cuts) > 0:
        array = steps_of(key, extent, cuts, -0.22, 0.18) * array
    return jnp.clip(array, min=-limit, max=limit).astype(kind)


def setup_inputs(seed: int = 0) -> dict:
    key_of = jax.random.split(jax.random.key(seed), 7)
    hidden_states = centred(key_of[0], (TOKENS, D), 1.0, 6.0, ((0, 8), (1, 4)))
    chosen_experts_keys = jax.random.split(jax.random.fold_in(key_of[1], 1), TOKENS // TOK_DEV)
    chosen_experts_turns = jax.random.permutation(jax.random.fold_in(key_of[1], 3), TOKENS // TOK_DEV)
    chosen_experts = jax.vmap(lambda own, number: assign_block(jax.random.fold_in(key_of[1], 2), own, number, TOK_DEV, EXPERTS, TOP, CAP, 2))(chosen_experts_keys, chosen_experts_turns).reshape((TOKENS, TOP))
    choice_weights = jnp.clip(0.2 + 0.8 * jax.random.uniform(key_of[2], (TOKENS, TOP), jnp.float32) ** steps_of(key_of[2], (TOKENS, TOP), ((0, 8),), -0.2, 0.2), 0.2, 1.0)
    gate_proj = centred(key_of[3], (EXPERTS, D, FF), D ** -0.5, 0.09375, ((0, 4), (2, 8)))
    up_proj = centred(key_of[4], (EXPERTS, D, FF), D ** -0.5, 0.09375, ((0, 4), (2, 8)))
    down_proj = centred(key_of[5], (EXPERTS, FF, D), FF ** -0.5, 0.0625, ((0, 4), (1, 2), (2, 4)))
    return {"hidden_states": hidden_states, "chosen_experts": chosen_experts, "choice_weights": choice_weights, "gate_proj": gate_proj, "up_proj": up_proj, "down_proj": down_proj}


def reference(hidden_states, chosen_experts, choice_weights, gate_proj, up_proj, down_proj):
    row_limit = N_DP * EXPERTS * CAP

    def expert_step(totals, expert):
        picked = chosen_experts == expert
        chosen = jnp.any(picked, axis=1)
        weight_row = jnp.sum(jnp.where(picked, choice_weights, jnp.float32(0.0)), axis=1)
        ranking = jnp.where(chosen, 0, 1).astype(jnp.int32)
        order = jnp.argsort(ranking, stable=True)[:row_limit].astype(jnp.int32)
        gathered = hidden_states[order]
        gate_part = jnp.dot(gathered, gate_proj[expert], preferred_element_type=jnp.float32)
        up_part = jnp.dot(gathered, up_proj[expert], preferred_element_type=jnp.float32)
        activated = (jax.nn.silu(gate_part) * up_part).astype(jnp.bfloat16)
        out_rows = jnp.dot(activated, down_proj[expert], preferred_element_type=jnp.float32)
        out_rows = lax.optimization_barrier(out_rows.astype(jnp.bfloat16)).astype(jnp.float32)
        scale_rows = jnp.where(chosen[order], weight_row[order], jnp.float32(0.0))
        totals = totals.at[order].add(out_rows * scale_rows[:, None])
        return totals, None

    start_sums = jnp.zeros((TOKENS, D), jnp.float32)
    totals, ignored = lax.scan(expert_step, start_sums, jnp.arange(EXPERTS, dtype=jnp.int32))
    return totals.astype(jnp.bfloat16)
```

```python
import functools

import jax
import jax.numpy as jnp
from jax import lax
from jax.experimental import pallas as pl
from jax.experimental.pallas import tpu as pltpu
from jax.sharding import PartitionSpec as P

CAP = 16
HOP = 2
CHUNKS = 2
MESH = pl.DeviceIdType.MESH


def kernel(
    nd, ne, nt,
    hidden_ref, ids_ref, weights_ref, gate_hbm, up_hbm, down_hbm, out_ref,
    packed, feats, acts, gate_w, up_w, down_w, gate_acc, up_acc, down_acc,
    outgoing, returned, table,
    w_sem, a2a_send, a2a_recv, z_send, z_recv, y_send, y_recv, ret_send, ret_recv,
):
    d, e, t = lax.axis_index("dp"), lax.axis_index("expert"), lax.axis_index("tensor")
    tokens, width = hidden_ref.shape
    slots = ne * CAP
    units = gate_w.shape[2]
    part = ne // CHUNKS
    tile_u = min(256, units)
    tile_f = min(256, width)

    def weight_copies(s):
        rows_f = pl.ds(pl.multiple_of(s * width, width), width)
        rows_u = pl.ds(pl.multiple_of(s * units, units), units)
        return (
            pltpu.make_async_copy(gate_hbm.at[0, rows_f], gate_w.at[s], w_sem.at[0, s]),
            pltpu.make_async_copy(up_hbm.at[0, rows_f], up_w.at[s], w_sem.at[1, s]),
            pltpu.make_async_copy(down_hbm.at[0, rows_u], down_w.at[s], w_sem.at[2, s]),
        )

    order = [0]
    for k in range(1, nt):
        order.append((k + 1) // 2 if k % 2 else nt - k // 2)
    for k in order:
        for copy in weight_copies(lax.rem(t + k, nt))[:2]:
            copy.start()
    for k in order:
        weight_copies(lax.rem(t + k, nt))[2].start()

    barrier = pltpu.get_barrier_semaphore()
    for j in range(nd):
        for k in range(ne):
            if j or k:
                pl.semaphore_signal(
                    barrier, inc=1, device_id_type=MESH,
                    device_id=(lax.rem(d + j, nd), lax.rem(e + k, ne), t),
                )
    for k in range(1, nt):
        pl.semaphore_signal(
            barrier, inc=1, device_id=(d, e, lax.rem(t + k, nt)), device_id_type=MESH
        )

    slot = lax.broadcasted_iota(jnp.int32, (tokens, slots), 1)
    slot_expert = lax.shift_right_logical(slot, CAP.bit_length() - 1)
    slot_place = slot - slot_expert * CAP
    named = jnp.zeros((tokens, slots), jnp.float32)
    weighted = jnp.zeros((tokens, slots), jnp.float32)
    for column in range(ids_ref.shape[1]):
        match = ids_ref[:, column : column + 1] == slot_expert
        named = jnp.where(match, 1.0, named)
        weighted = jnp.where(match, weights_ref[:, column : column + 1], weighted)
    earlier = lax.broadcasted_iota(jnp.int32, (tokens, tokens), 0) > (
        lax.broadcasted_iota(jnp.int32, (tokens, tokens), 1)
    )
    position = jnp.dot(
        jnp.where(earlier, 1.0, 0.0).astype(jnp.bfloat16),
        named.astype(jnp.bfloat16),
        preferred_element_type=jnp.float32,
    )
    placing = jnp.where(position == slot_place.astype(jnp.float32), named, 0.0)
    weighted = weighted * placing
    high = weighted.astype(jnp.bfloat16)
    rest = weighted - high.astype(jnp.float32)
    middle = rest.astype(jnp.bfloat16)
    table[0:tokens, :] = high
    table[tokens : 2 * tokens, :] = middle
    table[2 * tokens :, :] = (rest - middle.astype(jnp.float32)).astype(jnp.bfloat16)
    packed[...] = (
        lax.dot_general(
            placing.astype(jnp.bfloat16), hidden_ref[...], (((0,), (0,)), ((), ())),
            preferred_element_type=jnp.float32,
        )
        .astype(jnp.bfloat16)
        .reshape(ne, CAP, width)
    )
    pl.semaphore_wait(barrier, nd * ne + nt - 2)

    def a2a_copy(k):
        return pltpu.make_async_remote_copy(
            src_ref=packed.at[lax.rem(e + k, ne)],
            dst_ref=feats.at[d, t, e],
            send_sem=a2a_send.at[k],
            recv_sem=a2a_recv.at[e],
            device_id=(d, lax.rem(e + k, ne), t),
            device_id_type=MESH,
        )

    for k in range(1, ne):
        a2a_copy(k).start()
    feats[d, t, e] = packed[e]
    for k in range(1, ne):
        source = lax.rem(e + k, ne)
        pltpu.make_async_remote_copy(
            src_ref=packed.at[0],
            dst_ref=feats.at[d, t, source],
            send_sem=a2a_send.at[k],
            recv_sem=a2a_recv.at[source],
            device_id=(d, source, t),
            device_id_type=MESH,
        ).wait_recv()

    def z_copy(phase, ref, s, c, side, dist, hop):
        block = ref.at[s, pl.ds(c * part, part)]
        return pltpu.make_async_remote_copy(
            src_ref=block,
            dst_ref=block,
            send_sem=z_send.at[phase, c, side, dist // HOP, hop - 1],
            recv_sem=z_recv.at[phase, c, s],
            device_id=(d, e, t + hop * (1 - 2 * side)),
            device_id_type=MESH,
        )

    def for_targets(side, dist, act):
        step = 1 - 2 * side
        s = t - step * dist
        for hop in range(1, HOP + 1):
            to = t + step * hop

            @pl.when((s >= 0) & (s < nt) & (to >= 0) & (to < nt))
            def _():
                act(s, hop)

    def z_forward(phase, ref, side, dist, c):
        if dist % HOP == 0:
            for_targets(
                side, dist,
                lambda s, hop: z_copy(phase, ref, s, c, side, dist, hop).start(),
            )

    def z_drain(phase, ref):
        for c in range(CHUNKS):
            for side in range(2):
                for dist in range(0, nt, HOP):
                    for_targets(
                        side, dist,
                        lambda s, hop: z_copy(phase, ref, s, c, side, dist, hop).wait_send(),
                    )

    def z_arrive(phase, ref, s, c):
        z_copy(phase, ref, s, c, 0, 0, 1).wait_recv()

    def y_copy(j, b, s, c):
        block = feats.at[b, s, pl.ds(c * part, part)]
        return pltpu.make_async_remote_copy(
            src_ref=block,
            dst_ref=block,
            send_sem=y_send.at[j, s, c],
            recv_sem=y_recv.at[b, s, c],
            device_id=(lax.rem(d + j, nd), e, t),
            device_id_type=MESH,
        )

    def y_spread(s, c):
        for j in range(1, nd):
            y_copy(j, d, s, c).start()

    def gate_up(b, s, first):
        @pl.loop(0, units // tile_u)
        def _(i):
            columns = pl.ds(pl.multiple_of(i * tile_u, tile_u), tile_u)
            rows = feats[b, s].reshape(slots, width)
            gate = jnp.dot(rows, gate_w[s, :, columns], preferred_element_type=jnp.float32)
            up = jnp.dot(rows, up_w[s, :, columns], preferred_element_type=jnp.float32)
            if first is True:
                gate_acc[:, columns] = gate
                up_acc[:, columns] = up
            else:
                gate_acc[:, columns] += gate
                up_acc[:, columns] += up

    def activate(b):
        @pl.loop(0, units // tile_u)
        def _(i):
            columns = pl.ds(pl.multiple_of(i * tile_u, tile_u), tile_u)
            gate = gate_acc[:, columns]
            value = gate / (1.0 + jnp.exp(-gate)) * up_acc[:, columns]
            acts[b, t, :, :, columns] = value.astype(jnp.bfloat16).reshape(ne, CAP, tile_u)

    def down(b, s, first):
        @pl.loop(0, width // tile_f)
        def _(i):
            columns = pl.ds(pl.multiple_of(i * tile_f, tile_f), tile_f)
            rows = acts[b, s].reshape(slots, units)
            value = jnp.dot(rows, down_w[s, :, columns], preferred_element_type=jnp.float32)
            if first:
                down_acc[:, columns] = value
            else:
                down_acc[:, columns] += value

    def at_distance(dist, act):
        for side in range(2):
            s = t - (1 - 2 * side) * dist

            @pl.when((s >= 0) & (s < nt))
            def _():
                act(side, s)

    own = feats.at[d]
    for c in range(CHUNKS):
        z_forward(0, own, 0, 0, c)
        z_forward(0, own, 1, 0, c)
        y_spread(t, c)

    def weights_arrive(s):
        for copy in weight_copies(s)[:2]:
            copy.wait()

    weights_arrive(t)
    gate_up(d, t, True)
    for dist in range(1, nt):
        def take(side, s):
            for c in range(CHUNKS):
                z_arrive(0, own, s, c)
                z_forward(0, own, side, dist, c)
                y_spread(s, c)

        def use(side, s):
            weights_arrive(s)
            gate_up(d, s, False)

        at_distance(dist, take)
        at_distance(dist, use)
    activate(d)
    for c in range(CHUNKS):
        for side in range(2):
            z_forward(1, acts.at[d], side, 0, c)

    def other_rows(j, carry):
        b = lax.rem(d + j, nd)

        def arrive(s):
            for c in range(CHUNKS):
                y_copy(j, b, s, c).wait_recv()

        arrive(t)
        gate_up(b, t, True)

        def shard(k, carry):
            s = lax.rem(t + k, nt)
            arrive(s)
            gate_up(b, s, False)
            return carry

        lax.fori_loop(1, nt, shard, 0)
        activate(b)
        for c in range(CHUNKS):
            for side in range(2):
                z_forward(1 + j, acts.at[b], side, 0, c)
        return carry

    lax.fori_loop(1, nd, other_rows, 0)

    for k in range(nt):
        weight_copies(lax.rem(t + k, nt))[2].wait()

    def return_copy(j, b, k):
        to = lax.rem(e + k, ne)
        return pltpu.make_async_remote_copy(
            src_ref=outgoing.at[b, to],
            dst_ref=returned.at[d, e],
            send_sem=ret_send.at[j, k],
            recv_sem=ret_recv.at[d, e],
            device_id=(b, to, t),
            device_id_type=MESH,
        )

    def finish(j, carry):
        b = lax.rem(d + j, nd)
        ref = acts.at[b]
        down(b, t, True)
        for dist in range(1, nt):
            def take(side, s):
                for c in range(CHUNKS):
                    z_arrive(1 + j, ref, s, c)
                    z_forward(1 + j, ref, side, dist, c)

            at_distance(dist, take)
            at_distance(dist, lambda side, s: down(b, s, False))
        outgoing[b] = down_acc[...].astype(jnp.bfloat16).reshape(ne, CAP, width)
        for k in range(1, ne):
            return_copy(j, b, k).start()

        @pl.when(j == 0)
        def _():
            returned[d, e] = outgoing[d, e]

        @pl.when(j > 0)
        def _():
            return_copy(j, b, 0).start()

        return carry

    lax.fori_loop(0, nd, finish, 0)

    for j in range(nd):
        for k in range(ne):
            if j or k:
                b, source = lax.rem(d + j, nd), lax.rem(e + k, ne)
                pltpu.make_async_remote_copy(
                    src_ref=outgoing.at[0, 0],
                    dst_ref=returned.at[b, source],
                    send_sem=ret_send.at[j, k],
                    recv_sem=ret_recv.at[b, source],
                    device_id=(b, source, t),
                    device_id_type=MESH,
                ).wait_recv()
    total = jnp.zeros((table.shape[0], width), jnp.float32)
    for b in range(nd):
        total += jnp.dot(
            table[...], returned[b].reshape(slots, width), preferred_element_type=jnp.float32
        )
    out_ref[...] = (
        total[0:tokens] + total[tokens : 2 * tokens] + total[2 * tokens :]
    ).astype(jnp.bfloat16)

    for k in range(1, ne):
        a2a_copy(k).wait_send()
    for j in range(1, nd):
        for s in range(nt):
            for c in range(CHUNKS):
                y_copy(j, d, s, c).wait_send()
    z_drain(0, own)

    def drain(j, carry):
        b = lax.rem(d + j, nd)
        z_drain(1 + j, acts.at[b])
        for k in range(1, ne):
            return_copy(j, b, k).wait_send()

        @pl.when(j > 0)
        def _():
            return_copy(j, b, 0).wait_send()

        return carry

    lax.fori_loop(0, nd, drain, 0)


def body(mesh, hidden_states, chosen_experts, choice_weights, gate_proj, up_proj, down_proj):
    nd, ne, nt = mesh.shape["dp"], mesh.shape["expert"], mesh.shape["tensor"]
    tokens, width = hidden_states.shape
    units = gate_proj.shape[2]
    slots = ne * CAP
    vmem = pl.BlockSpec(memory_space=pltpu.VMEM)
    hbm = pl.BlockSpec(memory_space=pl.ANY)
    bf16, f32, dma = jnp.bfloat16, jnp.float32, pltpu.SemaphoreType.DMA
    lots = (nt + HOP - 1) // HOP
    return pl.pallas_call(
        functools.partial(kernel, nd, ne, nt),
        out_shape=jax.ShapeDtypeStruct((tokens, width), bf16),
        in_specs=[vmem, vmem, vmem, hbm, hbm, hbm],
        out_specs=vmem,
        scratch_shapes=[
            pltpu.VMEM((ne, CAP, width), bf16),
            pltpu.VMEM((nd, nt, ne, CAP, width), bf16),
            pltpu.VMEM((nd, nt, ne, CAP, units), bf16),
            pltpu.VMEM((nt, width, units), bf16),
            pltpu.VMEM((nt, width, units), bf16),
            pltpu.VMEM((nt, units, width), bf16),
            pltpu.VMEM((slots, units), f32),
            pltpu.VMEM((slots, units), f32),
            pltpu.VMEM((slots, width), f32),
            pltpu.VMEM((nd, ne, CAP, width), bf16),
            pltpu.VMEM((nd, ne, CAP, width), bf16),
            pltpu.VMEM((3 * tokens, slots), bf16),
            dma((3, nt)),
            dma((ne,)),
            dma((ne,)),
            dma((1 + nd, CHUNKS, 2, lots, HOP)),
            dma((1 + nd, CHUNKS, nt)),
            dma((nd, nt, CHUNKS)),
            dma((nd, nt, CHUNKS)),
            dma((nd, ne)),
            dma((nd, ne)),
        ],
        compiler_params=pltpu.CompilerParams(
            collective_id=0, has_side_effects=True, vmem_limit_bytes=48 << 20
        ),
        name="experts",
    )(hidden_states, chosen_experts, choice_weights, gate_proj, up_proj, down_proj)


def solution(mesh):
    in_specs = (
        P(("dp", "expert"), "tensor"),
        P(("dp", "expert"), None),
        P(("dp", "expert"), None),
        P("expert", None, ("dp", "tensor")),
        P("expert", None, ("dp", "tensor")),
        P("expert", "dp", "tensor"),
    )
    out_specs = P(("dp", "expert"), "tensor")
    return jax.shard_map(
        functools.partial(body, mesh), mesh=mesh, in_specs=in_specs, out_specs=out_specs,
        check_vma=False,
    )
```

```python
import functools

import jax
import jax.numpy as jnp
from jax import lax
from jax.experimental import pallas as pl
from jax.experimental.pallas import tpu as pltpu
from jax.sharding import PartitionSpec as P

CAP = 16
TOKEN_HOP = 2
UNIT_HOP = 1
CHUNKS = 2
TILE = 1024
MESH = pl.DeviceIdType.MESH


def kernel(
    nd, ne, nt,
    hidden_hbm, ids_hbm, weights_hbm, gate_hbm, up_hbm, down_hbm, out_ref,
    tokens_in, ids_ref, weights_ref, packed, feats, acts, gate_w, up_w, down_w,
    gate_acc, up_acc, down_acc, outgoing, returned, table,
    in_sem, w_sem, x_send, x_recv, z_send, z_recv, u_send, u_recv,
    y_send, y_recv, ret_send, ret_recv,
):
    d, e, t = lax.axis_index("dp"), lax.axis_index("expert"), lax.axis_index("tensor")
    tokens, width = tokens_in.shape[1:]
    slots = ne * CAP
    units = gate_w.shape[2]
    part = ne // CHUNKS
    tile_u = min(TILE, units)
    tile_f = min(TILE, width)

    barrier = pltpu.get_barrier_semaphore()
    for j in range(nd):
        for k in range(ne):
            if j or k:
                pl.semaphore_signal(
                    barrier, inc=1, device_id_type=MESH,
                    device_id=(lax.rem(d + j, nd), lax.rem(e + k, ne), t),
                )
    for k in range(1, nt):
        pl.semaphore_signal(
            barrier, inc=1, device_id=(d, e, lax.rem(t + k, nt)), device_id_type=MESH
        )
    inputs = (
        pltpu.make_async_copy(ids_hbm, ids_ref, in_sem.at[0]),
        pltpu.make_async_copy(weights_hbm, weights_ref, in_sem.at[1]),
        pltpu.make_async_copy(hidden_hbm, tokens_in.at[t], in_sem.at[2]),
    )
    for copy in inputs:
        copy.start()

    def weight_copy(i, s):
        size = units if i == 2 else width
        source = (gate_hbm, up_hbm, down_hbm)[i]
        return pltpu.make_async_copy(
            source.at[0, pl.ds(pl.multiple_of(s * size, size), size)],
            (gate_w, up_w, down_w)[i].at[s],
            w_sem.at[i, s],
        )

    order = [0]
    for k in range(1, nt):
        order.append((k + 1) // 2 if k % 2 else nt - k // 2)
    for k in order:
        weight_copy(0, lax.rem(t + k, nt)).start()
        weight_copy(1, lax.rem(t + k, nt)).start()
    for k in order:
        weight_copy(2, lax.rem(t + k, nt)).start()

    for copy in inputs:
        copy.wait()
    slot = lax.broadcasted_iota(jnp.int32, (slots, tokens), 0)
    slot_expert = lax.shift_right_logical(slot, CAP.bit_length() - 1)
    slot_place = slot - slot_expert * CAP
    named = jnp.zeros((slots, tokens), jnp.float32)
    weighted = jnp.zeros((slots, tokens), jnp.float32)
    for row in range(ids_ref.shape[0]):
        match = ids_ref[row : row + 1, :] == slot_expert
        named = jnp.where(match, 1.0, named)
        weighted = jnp.where(match, weights_ref[row : row + 1, :], weighted)
    earlier = lax.broadcasted_iota(jnp.int32, (tokens, tokens), 0) < (
        lax.broadcasted_iota(jnp.int32, (tokens, tokens), 1)
    )
    position = jnp.dot(
        named.astype(jnp.bfloat16),
        jnp.where(earlier, 1.0, 0.0).astype(jnp.bfloat16),
        preferred_element_type=jnp.float32,
    )
    placing = jnp.where(position == slot_place.astype(jnp.float32), named, 0.0)
    weighted = weighted * placing
    placing = placing.astype(jnp.bfloat16)
    high = weighted.astype(jnp.bfloat16)
    rest = weighted - high.astype(jnp.float32)
    middle = rest.astype(jnp.bfloat16)
    table[0] = high
    table[1] = middle
    table[2] = (rest - middle.astype(jnp.float32)).astype(jnp.bfloat16)
    table[3] = placing

    def x_copy(s, k):
        return pltpu.make_async_remote_copy(
            src_ref=packed.at[s, lax.rem(e + k, ne)],
            dst_ref=feats.at[d, s, e],
            send_sem=x_send.at[s, k],
            recv_sem=x_recv.at[s, e],
            device_id=(d, lax.rem(e + k, ne), t),
            device_id_type=MESH,
        )

    def x_spread(s):
        packed[s] = (
            jnp.dot(table[3], tokens_in[s], preferred_element_type=jnp.float32)
            .astype(jnp.bfloat16)
            .reshape(ne, CAP, width)
        )
        for k in range(1, ne):
            x_copy(s, k).start()
        feats[d, s, e] = packed[s, e]

    def x_arrive(s):
        for k in range(1, ne):
            source = lax.rem(e + k, ne)
            pltpu.make_async_remote_copy(
                src_ref=packed.at[s, source],
                dst_ref=feats.at[d, s, source],
                send_sem=x_send.at[s, k],
                recv_sem=x_recv.at[s, source],
                device_id=(d, source, t),
                device_id_type=MESH,
            ).wait_recv()

    class Line:
        def __init__(self, hop, chunks, block, send_sem, recv_sem):
            self.hop, self.chunks, self.block = hop, chunks, block
            self.send_sem, self.recv_sem = send_sem, recv_sem

        def copy(self, s, c, side, dist, hop):
            block = self.block(s, c)
            return pltpu.make_async_remote_copy(
                src_ref=block,
                dst_ref=block,
                send_sem=self.send_sem(c, side, dist // self.hop, hop - 1),
                recv_sem=self.recv_sem(c, s),
                device_id=(d, e, t + hop * (1 - 2 * side)),
                device_id_type=MESH,
            )

        def targets(self, side, dist, act):
            step = 1 - 2 * side
            s = t - step * dist
            for hop in range(1, self.hop + 1):
                to = t + step * hop

                @pl.when((s >= 0) & (s < nt) & (to >= 0) & (to < nt))
                def _():
                    act(s, hop)

        def forward(self, side, dist, c):
            if dist % self.hop == 0:
                self.targets(
                    side, dist, lambda s, hop: self.copy(s, c, side, dist, hop).start()
                )

        def send_own(self):
            for c in range(self.chunks):
                for side in range(2):
                    self.forward(side, 0, c)

        def arrive(self, side, dist, s):
            for c in range(self.chunks):
                self.copy(s, c, 0, 0, 1).wait_recv()
                self.forward(side, dist, c)

        def drain(self):
            for c in range(self.chunks):
                for side in range(2):
                    for dist in range(0, nt, self.hop):
                        self.targets(
                            side, dist,
                            lambda s, hop: self.copy(s, c, side, dist, hop).wait_send(),
                        )

    token_line = Line(
        TOKEN_HOP, 1, lambda s, c: tokens_in.at[s],
        lambda c, side, i, h: z_send.at[side, i, h], lambda c, s: z_recv.at[s],
    )

    def unit_line(j, b):
        return Line(
            UNIT_HOP, CHUNKS, lambda s, c: acts.at[b, s, pl.ds(c * part, part)],
            lambda c, side, i, h: u_send.at[j, c, side, i, h],
            lambda c, s: u_recv.at[j, c, s],
        )

    def y_copy(j, b, s, c):
        block = feats.at[b, s, pl.ds(c * part, part)]
        return pltpu.make_async_remote_copy(
            src_ref=block,
            dst_ref=block,
            send_sem=y_send.at[j, s, c],
            recv_sem=y_recv.at[b, s, c],
            device_id=(lax.rem(d + j, nd), e, t),
            device_id_type=MESH,
        )

    def y_spread(s, c):
        for j in range(1, nd):
            y_copy(j, d, s, c).start()

    def gate_up(b, s, first):
        @pl.loop(0, units // tile_u)
        def _(i):
            columns = pl.ds(pl.multiple_of(i * tile_u, tile_u), tile_u)
            rows = feats[b, s].reshape(slots, width)
            gate = jnp.dot(rows, gate_w[s, :, columns], preferred_element_type=jnp.float32)
            up = jnp.dot(rows, up_w[s, :, columns], preferred_element_type=jnp.float32)
            if first is True:
                gate_acc[:, columns] = gate
                up_acc[:, columns] = up
            else:
                gate_acc[:, columns] += gate
                up_acc[:, columns] += up

    def activate(b):
        @pl.loop(0, units // tile_u)
        def _(i):
            columns = pl.ds(pl.multiple_of(i * tile_u, tile_u), tile_u)
            gate = gate_acc[:, columns]
            value = gate / (1.0 + jnp.exp(-gate)) * up_acc[:, columns]
            acts[b, t, :, :, columns] = value.astype(jnp.bfloat16).reshape(ne, CAP, tile_u)

    def down(b, s, first):
        @pl.loop(0, width // tile_f)
        def _(i):
            columns = pl.ds(pl.multiple_of(i * tile_f, tile_f), tile_f)
            rows = acts[b, s].reshape(slots, units)
            value = jnp.dot(rows, down_w[s, :, columns], preferred_element_type=jnp.float32)
            if first:
                down_acc[:, columns] = value
            else:
                down_acc[:, columns] += value

    def at_distance(dist, act):
        for side in range(2):
            s = t - (1 - 2 * side) * dist

            @pl.when((s >= 0) & (s < nt))
            def _():
                act(side, s)

    pl.semaphore_wait(barrier, nd * ne + nt - 2)
    token_line.send_own()
    x_spread(t)

    def use(s, first):
        x_arrive(s)
        for c in range(CHUNKS):
            y_spread(s, c)
        weight_copy(0, s).wait()
        weight_copy(1, s).wait()
        gate_up(d, s, first)

    for dist in range(1, nt + 1):
        if dist < nt:
            def take(side, s):
                token_line.arrive(side, dist, s)
                x_spread(s)

            at_distance(dist, take)
        if dist == 1:
            use(t, True)
        else:
            at_distance(dist - 1, lambda side, s: use(s, False))
    activate(d)
    unit_line(0, d).send_own()

    def other_rows(j, carry):
        b = lax.rem(d + j, nd)

        def arrive(s):
            for c in range(CHUNKS):
                y_copy(j, b, s, c).wait_recv()

        arrive(t)
        gate_up(b, t, True)

        def shard(k, carry):
            s = lax.rem(t + k, nt)
            arrive(s)
            gate_up(b, s, False)
            return carry

        lax.fori_loop(1, nt, shard, 0)
        activate(b)
        unit_line(j, b).send_own()
        return carry

    lax.fori_loop(1, nd, other_rows, 0)

    for k in range(nt):
        weight_copy(2, lax.rem(t + k, nt)).wait()

    def return_copy(j, b, k):
        to = lax.rem(e + k, ne)
        return pltpu.make_async_remote_copy(
            src_ref=outgoing.at[b, to],
            dst_ref=returned.at[d, e],
            send_sem=ret_send.at[j, k],
            recv_sem=ret_recv.at[d, e],
            device_id=(b, to, t),
            device_id_type=MESH,
        )

    def finish(j, carry):
        b = lax.rem(d + j, nd)
        line = unit_line(j, b)
        down(b, t, True)
        for dist in range(1, nt):
            at_distance(dist, lambda side, s: line.arrive(side, dist, s))
            at_distance(dist, lambda side, s: down(b, s, False))
        outgoing[b] = down_acc[...].astype(jnp.bfloat16).reshape(ne, CAP, width)
        for k in range(1, ne):
            return_copy(j, b, k).start()

        @pl.when(j == 0)
        def _():
            returned[d, e] = outgoing[d, e]

        @pl.when(j > 0)
        def _():
            return_copy(j, b, 0).start()

        return carry

    lax.fori_loop(0, nd, finish, 0)

    for j in range(nd):
        for k in range(ne):
            if j or k:
                b, source = lax.rem(d + j, nd), lax.rem(e + k, ne)
                pltpu.make_async_remote_copy(
                    src_ref=outgoing.at[0, 0],
                    dst_ref=returned.at[b, source],
                    send_sem=ret_send.at[j, k],
                    recv_sem=ret_recv.at[b, source],
                    device_id=(b, source, t),
                    device_id_type=MESH,
                ).wait_recv()
    total = jnp.zeros((tokens, width), jnp.float32)
    for b in range(nd):
        rows = returned[b].reshape(slots, width)
        for i in range(3):
            total += lax.dot_general(
                table[i], rows, (((0,), (0,)), ((), ())), preferred_element_type=jnp.float32
            )
    out_ref[...] = total.astype(jnp.bfloat16)

    for s in range(nt):
        for k in range(1, ne):
            x_copy(s, k).wait_send()
    for j in range(1, nd):
        for s in range(nt):
            for c in range(CHUNKS):
                y_copy(j, d, s, c).wait_send()
    token_line.drain()

    def drain(j, carry):
        b = lax.rem(d + j, nd)
        unit_line(j, b).drain()
        for k in range(1, ne):
            return_copy(j, b, k).wait_send()

        @pl.when(j > 0)
        def _():
            return_copy(j, b, 0).wait_send()

        return carry

    lax.fori_loop(0, nd, drain, 0)


def body(mesh, hidden_states, chosen_experts, choice_weights, gate_proj, up_proj, down_proj):
    nd, ne, nt = mesh.shape["dp"], mesh.shape["expert"], mesh.shape["tensor"]
    tokens, width = hidden_states.shape
    units = gate_proj.shape[2]
    slots = ne * CAP
    vmem = pl.BlockSpec(memory_space=pltpu.VMEM)
    hbm = pl.BlockSpec(memory_space=pl.ANY)
    bf16, f32, dma = jnp.bfloat16, jnp.float32, pltpu.SemaphoreType.DMA
    token_sends = (2, pl.cdiv(nt, TOKEN_HOP), TOKEN_HOP)
    unit_sends = (nd, CHUNKS, 2, pl.cdiv(nt, UNIT_HOP), UNIT_HOP)
    return pl.pallas_call(
        functools.partial(kernel, nd, ne, nt),
        out_shape=jax.ShapeDtypeStruct((tokens, width), bf16),
        in_specs=[hbm] * 6,
        out_specs=vmem,
        scratch_shapes=[
            pltpu.VMEM((nt, tokens, width), bf16),
            pltpu.VMEM(chosen_experts.shape[::-1], jnp.int32),
            pltpu.VMEM(choice_weights.shape[::-1], f32),
            pltpu.VMEM((nt, ne, CAP, width), bf16),
            pltpu.VMEM((nd, nt, ne, CAP, width), bf16),
            pltpu.VMEM((nd, nt, ne, CAP, units), bf16),
            pltpu.VMEM((nt, width, units), bf16),
            pltpu.VMEM((nt, width, units), bf16),
            pltpu.VMEM((nt, units, width), bf16),
            pltpu.VMEM((slots, units), f32),
            pltpu.VMEM((slots, units), f32),
            pltpu.VMEM((slots, width), f32),
            pltpu.VMEM((nd, ne, CAP, width), bf16),
            pltpu.VMEM((nd, ne, CAP, width), bf16),
            pltpu.VMEM((4, slots, tokens), bf16),
            dma((3,)),
            dma((3, nt)),
            dma((nt, ne)),
            dma((nt, ne)),
            dma(token_sends),
            dma((nt,)),
            dma(unit_sends),
            dma((nd, CHUNKS, nt)),
            dma((nd, nt, CHUNKS)),
            dma((nd, nt, CHUNKS)),
            dma((nd, ne)),
            dma((nd, ne)),
        ],
        compiler_params=pltpu.CompilerParams(
            collective_id=0, has_side_effects=True, vmem_limit_bytes=48 << 20
        ),
        name="experts",
    )(hidden_states, chosen_experts.T, choice_weights.T, gate_proj, up_proj, down_proj)


def solution(mesh):
    in_specs = (
        P(("dp", "expert"), "tensor"),
        P(("dp", "expert"), None),
        P(("dp", "expert"), None),
        P("expert", None, ("dp", "tensor")),
        P("expert", None, ("dp", "tensor")),
        P("expert", "dp", "tensor"),
    )
    out_specs = P(("dp", "expert"), "tensor")
    return jax.shard_map(
        functools.partial(body, mesh), mesh=mesh, in_specs=in_specs, out_specs=out_specs,
        check_vma=False,
    )
```

```python
import functools

import jax
import jax.numpy as jnp
from jax import lax
from jax.experimental import pallas as pl
from jax.experimental.pallas import tpu as pltpu
from jax.sharding import PartitionSpec as P

CAP = 16
TOKEN_HOP = 1
UNIT_HOP = 2
CHUNKS = 2
TILE = 1024
MESH = pl.DeviceIdType.MESH


def kernel(
    nd, ne, nt,
    hidden_hbm, ids_hbm, weights_hbm, gate_hbm, up_hbm, down_hbm, out_ref,
    tokens_in, ids_ref, weights_ref, packed, feats, acts, gate_w, up_w, down_w,
    gate_acc, up_acc, down_acc, outgoing, returned, table,
    in_sem, w_sem, x_send, x_recv, z_send, z_recv, u_send, u_recv,
    y_send, y_recv, ret_send, ret_recv,
):
    d, e, t = lax.axis_index("dp"), lax.axis_index("expert"), lax.axis_index("tensor")
    tokens, width = tokens_in.shape[1:]
    slots = ne * CAP
    units = gate_w.shape[2]
    part = ne // CHUNKS
    tile_u = min(TILE, units)
    tile_f = min(TILE, width)

    barrier = pltpu.get_barrier_semaphore()
    for j in range(nd):
        for k in range(ne):
            if j or k:
                pl.semaphore_signal(
                    barrier, inc=1, device_id_type=MESH,
                    device_id=(lax.rem(d + j, nd), lax.rem(e + k, ne), t),
                )
    for k in range(1, nt):
        pl.semaphore_signal(
            barrier, inc=1, device_id=(d, e, lax.rem(t + k, nt)), device_id_type=MESH
        )
    inputs = (
        pltpu.make_async_copy(ids_hbm, ids_ref, in_sem.at[0]),
        pltpu.make_async_copy(weights_hbm, weights_ref, in_sem.at[1]),
        pltpu.make_async_copy(hidden_hbm, tokens_in.at[t], in_sem.at[2]),
    )
    for copy in inputs:
        copy.start()

    def weight_copy(i, s):
        size = units if i == 2 else width
        source = (gate_hbm, up_hbm, down_hbm)[i]
        return pltpu.make_async_copy(
            source.at[0, pl.ds(pl.multiple_of(s * size, size), size)],
            (gate_w, up_w, down_w)[i].at[s],
            w_sem.at[i, s],
        )

    order = [0]
    for k in range(1, nt):
        order.append((k + 1) // 2 if k % 2 else nt - k // 2)
    for k in order:
        weight_copy(0, lax.rem(t + k, nt)).start()
        weight_copy(1, lax.rem(t + k, nt)).start()
    for k in order:
        weight_copy(2, lax.rem(t + k, nt)).start()

    for copy in inputs:
        copy.wait()
    slot = lax.broadcasted_iota(jnp.int32, (slots, tokens), 0)
    slot_expert = lax.shift_right_logical(slot, CAP.bit_length() - 1)
    slot_place = slot - slot_expert * CAP
    named = jnp.zeros((slots, tokens), jnp.float32)
    weighted = jnp.zeros((slots, tokens), jnp.float32)
    for row in range(ids_ref.shape[0]):
        match = ids_ref[row : row + 1, :] == slot_expert
        named = jnp.where(match, 1.0, named)
        weighted = jnp.where(match, weights_ref[row : row + 1, :], weighted)
    earlier = lax.broadcasted_iota(jnp.int32, (tokens, tokens), 0) < (
        lax.broadcasted_iota(jnp.int32, (tokens, tokens), 1)
    )
    position = jnp.dot(
        named.astype(jnp.bfloat16),
        jnp.where(earlier, 1.0, 0.0).astype(jnp.bfloat16),
        preferred_element_type=jnp.float32,
    )
    placing = jnp.where(position == slot_place.astype(jnp.float32), named, 0.0)
    weighted = weighted * placing
    placing = placing.astype(jnp.bfloat16)
    high = weighted.astype(jnp.bfloat16)
    rest = weighted - high.astype(jnp.float32)
    middle = rest.astype(jnp.bfloat16)
    table[0] = high
    table[1] = middle
    table[2] = (rest - middle.astype(jnp.float32)).astype(jnp.bfloat16)
    table[3] = placing

    def x_copy(s, k):
        return pltpu.make_async_remote_copy(
            src_ref=packed.at[s, lax.rem(e + k, ne)],
            dst_ref=feats.at[d, s, e],
            send_sem=x_send.at[s, k],
            recv_sem=x_recv.at[s, e],
            device_id=(d, lax.rem(e + k, ne), t),
            device_id_type=MESH,
        )

    def x_spread(s):
        packed[s] = (
            jnp.dot(table[3], tokens_in[s], preferred_element_type=jnp.float32)
            .astype(jnp.bfloat16)
            .reshape(ne, CAP, width)
        )
        for k in range(1, ne):
            x_copy(s, k).start()
        feats[d, s, e] = packed[s, e]

    def x_arrive(s):
        for k in range(1, ne):
            source = lax.rem(e + k, ne)
            pltpu.make_async_remote_copy(
                src_ref=packed.at[s, source],
                dst_ref=feats.at[d, s, source],
                send_sem=x_send.at[s, k],
                recv_sem=x_recv.at[s, source],
                device_id=(d, source, t),
                device_id_type=MESH,
            ).wait_recv()

    class Line:
        def __init__(self, hop, chunks, block, send_sem, recv_sem):
            self.hop, self.chunks, self.block = hop, chunks, block
            self.send_sem, self.recv_sem = send_sem, recv_sem

        def copy(self, s, c, side, dist, hop):
            block = self.block(s, c)
            return pltpu.make_async_remote_copy(
                src_ref=block,
                dst_ref=block,
                send_sem=self.send_sem(c, side, dist // self.hop, hop - 1),
                recv_sem=self.recv_sem(c, s),
                device_id=(d, e, t + hop * (1 - 2 * side)),
                device_id_type=MESH,
            )

        def targets(self, side, dist, act):
            step = 1 - 2 * side
            s = t - step * dist
            for hop in range(1, self.hop + 1):
                to = t + step * hop

                @pl.when((s >= 0) & (s < nt) & (to >= 0) & (to < nt))
                def _():
                    act(s, hop)

        def forward(self, side, dist, c):
            if dist % self.hop == 0:
                self.targets(
                    side, dist, lambda s, hop: self.copy(s, c, side, dist, hop).start()
                )

        def send_own(self):
            for c in range(self.chunks):
                for side in range(2):
                    self.forward(side, 0, c)

        def arrive(self, side, dist, s):
            for c in range(self.chunks):
                self.copy(s, c, 0, 0, 1).wait_recv()
                self.forward(side, dist, c)

        def drain(self):
            for c in range(self.chunks):
                for side in range(2):
                    for dist in range(0, nt, self.hop):
                        self.targets(
                            side, dist,
                            lambda s, hop: self.copy(s, c, side, dist, hop).wait_send(),
                        )

    token_line = Line(
        TOKEN_HOP, 1, lambda s, c: tokens_in.at[s],
        lambda c, side, i, h: z_send.at[side, i, h], lambda c, s: z_recv.at[s],
    )

    def unit_line(j, b):
        return Line(
            UNIT_HOP, CHUNKS, lambda s, c: acts.at[b, s, pl.ds(c * part, part)],
            lambda c, side, i, h: u_send.at[j, c, side, i, h],
            lambda c, s: u_recv.at[j, c, s],
        )

    def y_copy(j, b, s, c):
        block = feats.at[b, s, pl.ds(c * part, part)]
        return pltpu.make_async_remote_copy(
            src_ref=block,
            dst_ref=block,
            send_sem=y_send.at[j, s, c],
            recv_sem=y_recv.at[b, s, c],
            device_id=(lax.rem(d + j, nd), e, t),
            device_id_type=MESH,
        )

    def y_spread(s, c):
        for j in range(1, nd):
            y_copy(j, d, s, c).start()

    def gate_up(b, s, first):
        @pl.loop(0, units // tile_u)
        def _(i):
            columns = pl.ds(pl.multiple_of(i * tile_u, tile_u), tile_u)
            rows = feats[b, s].reshape(slots, width)
            gate = jnp.dot(rows, gate_w[s, :, columns], preferred_element_type=jnp.float32)
            up = jnp.dot(rows, up_w[s, :, columns], preferred_element_type=jnp.float32)
            if first is True:
                gate_acc[:, columns] = gate
                up_acc[:, columns] = up
            else:
                gate_acc[:, columns] += gate
                up_acc[:, columns] += up

    def activate(b):
        @pl.loop(0, units // tile_u)
        def _(i):
            columns = pl.ds(pl.multiple_of(i * tile_u, tile_u), tile_u)
            gate = gate_acc[:, columns]
            value = gate / (1.0 + jnp.exp(-gate)) * up_acc[:, columns]
            acts[b, t, :, :, columns] = value.astype(jnp.bfloat16).reshape(ne, CAP, tile_u)

    def down(b, s, first):
        @pl.loop(0, width // tile_f)
        def _(i):
            columns = pl.ds(pl.multiple_of(i * tile_f, tile_f), tile_f)
            rows = acts[b, s].reshape(slots, units)
            value = jnp.dot(rows, down_w[s, :, columns], preferred_element_type=jnp.float32)
            if first:
                down_acc[:, columns] = value
            else:
                down_acc[:, columns] += value

    def at_distance(dist, act):
        for side in range(2):
            s = t - (1 - 2 * side) * dist

            @pl.when((s >= 0) & (s < nt))
            def _():
                act(side, s)

    pl.semaphore_wait(barrier, nd * ne + nt - 2)
    token_line.send_own()
    x_spread(t)

    def use(s, first):
        x_arrive(s)
        for c in range(CHUNKS):
            y_spread(s, c)
        weight_copy(0, s).wait()
        weight_copy(1, s).wait()
        gate_up(d, s, first)

    for dist in range(1, nt + 1):
        if dist < nt:
            def take(side, s):
                token_line.arrive(side, dist, s)
                x_spread(s)

            at_distance(dist, take)
        if dist == 1:
            use(t, True)
        else:
            at_distance(dist - 1, lambda side, s: use(s, False))
    activate(d)
    unit_line(0, d).send_own()

    def return_copy(j, b, k):
        to = lax.rem(e + k, ne)
        return pltpu.make_async_remote_copy(
            src_ref=outgoing.at[b, to],
            dst_ref=returned.at[d, e],
            send_sem=ret_send.at[j, k],
            recv_sem=ret_recv.at[d, e],
            device_id=(b, to, t),
            device_id_type=MESH,
        )

    def finish(j, b):
        outgoing[b] = down_acc[...].astype(jnp.bfloat16).reshape(ne, CAP, width)
        for k in range(1, ne):
            return_copy(j, b, k).start()

        @pl.when(j == 0)
        def _():
            returned[d, e] = outgoing[d, e]

        @pl.when(j > 0)
        def _():
            return_copy(j, b, 0).start()

    def step(j, carry):
        b, before = lax.rem(d + j, nd), lax.rem(d + j - 1, nd)
        line = unit_line(j - 1, before)

        def pass_on(dist):
            at_distance(dist, lambda side, s: line.arrive(side, dist, s))

        for k in range(nt):
            s = lax.rem(t + order[k], nt)
            for c in range(CHUNKS):
                y_copy(j, b, s, c).wait_recv()
            gate_up(b, s, k == 0)
            if 0 < k < nt - 1:
                pass_on(k)
        activate(b)
        unit_line(j, b).send_own()

        @pl.when(j == 1)
        def _():
            for k in range(nt):
                weight_copy(2, lax.rem(t + k, nt)).wait()

        down(before, t, True)
        for dist in range(1, nt):
            if dist == nt - 1:
                pass_on(dist)
            at_distance(dist, lambda side, s: down(before, s, False))
        finish(j - 1, before)
        return carry

    lax.fori_loop(1, nd, step, 0)
    last = lax.rem(d + nd - 1, nd)
    line = unit_line(nd - 1, last)
    down(last, t, True)
    for dist in range(1, nt):
        at_distance(dist, lambda side, s: line.arrive(side, dist, s))
        at_distance(dist, lambda side, s: down(last, s, False))
    finish(nd - 1, last)

    for j in range(nd):
        for k in range(ne):
            if j or k:
                b, source = lax.rem(d + j, nd), lax.rem(e + k, ne)
                pltpu.make_async_remote_copy(
                    src_ref=outgoing.at[0, 0],
                    dst_ref=returned.at[b, source],
                    send_sem=ret_send.at[j, k],
                    recv_sem=ret_recv.at[b, source],
                    device_id=(b, source, t),
                    device_id_type=MESH,
                ).wait_recv()
    total = jnp.zeros((tokens, width), jnp.float32)
    for b in range(nd):
        rows = returned[b].reshape(slots, width)
        for i in range(3):
            total += lax.dot_general(
                table[i], rows, (((0,), (0,)), ((), ())), preferred_element_type=jnp.float32
            )
    out_ref[...] = total.astype(jnp.bfloat16)

    for s in range(nt):
        for k in range(1, ne):
            x_copy(s, k).wait_send()
    for j in range(1, nd):
        for s in range(nt):
            for c in range(CHUNKS):
                y_copy(j, d, s, c).wait_send()
    token_line.drain()

    def drain(j, carry):
        b = lax.rem(d + j, nd)
        unit_line(j, b).drain()
        for k in range(1, ne):
            return_copy(j, b, k).wait_send()

        @pl.when(j > 0)
        def _():
            return_copy(j, b, 0).wait_send()

        return carry

    lax.fori_loop(0, nd, drain, 0)


def body(mesh, hidden_states, chosen_experts, choice_weights, gate_proj, up_proj, down_proj):
    nd, ne, nt = mesh.shape["dp"], mesh.shape["expert"], mesh.shape["tensor"]
    tokens, width = hidden_states.shape
    units = gate_proj.shape[2]
    slots = ne * CAP
    vmem = pl.BlockSpec(memory_space=pltpu.VMEM)
    hbm = pl.BlockSpec(memory_space=pl.ANY)
    bf16, f32, dma = jnp.bfloat16, jnp.float32, pltpu.SemaphoreType.DMA
    token_sends = (2, pl.cdiv(nt, TOKEN_HOP), TOKEN_HOP)
    unit_sends = (nd, CHUNKS, 2, pl.cdiv(nt, UNIT_HOP), UNIT_HOP)
    return pl.pallas_call(
        functools.partial(kernel, nd, ne, nt),
        out_shape=jax.ShapeDtypeStruct((tokens, width), bf16),
        in_specs=[hbm] * 6,
        out_specs=vmem,
        scratch_shapes=[
            pltpu.VMEM((nt, tokens, width), bf16),
            pltpu.VMEM(chosen_experts.shape[::-1], jnp.int32),
            pltpu.VMEM(choice_weights.shape[::-1], f32),
            pltpu.VMEM((nt, ne, CAP, width), bf16),
            pltpu.VMEM((nd, nt, ne, CAP, width), bf16),
            pltpu.VMEM((nd, nt, ne, CAP, units), bf16),
            pltpu.VMEM((nt, width, units), bf16),
            pltpu.VMEM((nt, width, units), bf16),
            pltpu.VMEM((nt, units, width), bf16),
            pltpu.VMEM((slots, units), f32),
            pltpu.VMEM((slots, units), f32),
            pltpu.VMEM((slots, width), f32),
            pltpu.VMEM((nd, ne, CAP, width), bf16),
            pltpu.VMEM((nd, ne, CAP, width), bf16),
            pltpu.VMEM((4, slots, tokens), bf16),
            dma((3,)),
            dma((3, nt)),
            dma((nt, ne)),
            dma((nt, ne)),
            dma(token_sends),
            dma((nt,)),
            dma(unit_sends),
            dma((nd, CHUNKS, nt)),
            dma((nd, nt, CHUNKS)),
            dma((nd, nt, CHUNKS)),
            dma((nd, ne)),
            dma((nd, ne)),
        ],
        compiler_params=pltpu.CompilerParams(
            collective_id=0, has_side_effects=True, vmem_limit_bytes=48 << 20
        ),
        name="experts",
    )(hidden_states, chosen_experts.T, choice_weights.T, gate_proj, up_proj, down_proj)


def solution(mesh):
    in_specs = (
        P(("dp", "expert"), "tensor"),
        P(("dp", "expert"), None),
        P(("dp", "expert"), None),
        P("expert", None, ("dp", "tensor")),
        P("expert", None, ("dp", "tensor")),
        P("expert", "dp", "tensor"),
    )
    out_specs = P(("dp", "expert"), "tensor")
    return jax.shard_map(
        functools.partial(body, mesh), mesh=mesh, in_specs=in_specs, out_specs=out_specs,
        check_vma=False,
    )
```
